32 devices in a mesh: ctx: 8 (over y, x, core), ch: 4 (over z).
Axes of the slice: x: 2, y: 2, z: 4, core: 2. Of those that a mesh axis runs over, the one named last changes fastest.
Arguments:
- query: float32 [1024, 6144], P('ctx', 'ch'), may hold values from -6 to 6
- key_proj: float32 [1024, 6144], P('ctx', 'ch'), may hold values from -6 to 6
- value_proj: float32 [1024, 6144], P('ctx', 'ch'), may hold values from -6 to 6
- skip_gain: float32 [6144], P('ch'), may hold values from -4 to 4
- rates: float32 [384, 16], P('ch'), as said below
- residues: float32 [384, 16], P('ch')
- w_out: bfloat16 [6144, 8192], P('ch', 'ctx'), may hold values from -0.078125 to 0.078125
Outputs:
- projected_out: float32 [1024, 8192], P('ctx', 'ch')
The draws below stay inside these ranges and needn't reach their ends.
Inputs may be any that keep to these rules, and one draw needn't show every extreme that they name: `rates`: each rate is positive, from 0.3 / 1024 up to 1 / 24.
All inputs are finite; a program needn't handle non-finite values.
Results may differ from the reference program's by a relative error of at most 0.0029.
Values may be sent and summed in bfloat16 or wider, within the bound.
A program may use at most 192 MiB of HBM per device.

```python
import jax
import jax.numpy as jnp
from jax import lax

DO = 8192
DW = 6144
MODES = 16
TOK_DEV = 128
TOKENS = 1024
FILTERS = 384


def rate_table(key):
    base_key = jax.random.fold_in(key, 11)
    pick_key, spread_key = jax.random.split(base_key, 2)
    slow_cut = 1.0 / 3.0
    mid_cut = 2.0 / 3.0
    picker = jax.random.uniform(pick_key, (FILTERS, MODES), jnp.float32)
    spread = jax.random.uniform(spread_key, (FILTERS, MODES), jnp.float32)
    slow_low = jnp.log(0.3 / TOKENS)
    slow_high = jnp.log(2.0 / TOKENS)
    middle_low = jnp.log(0.125 / TOK_DEV)
    middle_high = jnp.log(1.0 / 48.0)
    fast_low = jnp.log(1.0 / 48.0)
    fast_high = jnp.log(1.0 / 24.0)
    slow_rate = jnp.exp(slow_low + spread * (slow_high - slow_low))
    middle_rate = jnp.exp(middle_low + spread * (middle_high - middle_low))
    fast_rate = jnp.exp(fast_low + spread * (fast_high - fast_low))
    chosen = jnp.where(picker < slow_cut, slow_rate, jnp.where(picker < mid_cut, middle_rate, fast_rate))
    return chosen.astype(jnp.float32)


def draw_rates(key, part):
    return rate_table(key)


def draw_residues(key, part):
    rate_values = rate_table(key)
    normal_part = jnp.clip(jax.random.normal(jax.random.fold_in(key, 23), (FILTERS, MODES), jnp.float32), -4.0, 4.0)
    return (normal_part * jnp.sqrt(2.0 * rate_values / MODES)).astype(jnp.float32)


def shard_levels(own_key, shape, cuts, smallest, largest):
    gain = 1.0
    for axis_at, blocks in cuts:
        draws = jax.random.uniform(jax.random.fold_in(jax.random.fold_in(own_key, 6), axis_at), (blocks,), jnp.float32, smallest / len(cuts), largest / len(cuts))
        gain = gain * jnp.repeat(jnp.exp(draws), shape[axis_at] // blocks).reshape((-1,) + (1,) * (len(shape) - 1 - axis_at))
    return gain


def normal_values(own_key, dims, scale, most, pieces=(), held_as=jnp.bfloat16):
    result = jax.random.normal(own_key, dims, jnp.float32) * scale
    if len(pieces) > 0:
        result = shard_levels(own_key, dims, pieces, -0.22, 0.18) * result
    return jnp.clip(result, min=-most, max=most).astype(held_as)


def setup_inputs(seed: int = 0) -> dict:
    splits = jax.random.split(jax.random.key(seed), 8)
    query = normal_values(splits[0], (TOKENS, DW), 1.0, 6.0, ((0, 8), (1, 4)), jnp.float32)
    key_proj = normal_values(splits[1], (TOKENS, DW), 1.0, 6.0, ((0, 8), (1, 4)), jnp.float32)
    value_proj = normal_values(splits[2], (TOKENS, DW), 1.0, 6.0, ((0, 8), (1, 4)), jnp.float32)
    skip_gain = normal_values(splits[3], (DW,), 1.0, 4.0, ((0, 4),), jnp.float32)
    rates = draw_rates(jax.random.fold_in(splits[7], 71), 0)
    residues = draw_residues(jax.random.fold_in(splits[7], 71), 0)
    w_out = normal_values(splits[6], (DW, DO), DW ** -0.5, 0.078125, ((0, 4), (1, 8)))
    return dict(query=query, key_proj=key_proj, value_proj=value_proj, skip_gain=skip_gain, rates=rates, residues=residues, w_out=w_out)


def reference(query, key_proj, value_proj, skip_gain, rates, residues, w_out):
    kv_prod = key_proj * value_proj
    seq_len = kv_prod.shape[0]
    filter_count = rates.shape[0]
    group_size = kv_prod.shape[1] // filter_count
    time_axis = jnp.arange(seq_len, dtype=jnp.float32)
    padded_len = 2 * seq_len

    def convolve_filter(operands):
        signal, rate_row, residue_row = operands
        taps = jnp.sum(residue_row[:, None] * jnp.exp(-rate_row[:, None] * time_axis[None, :]), axis=0)
        spectrum = jnp.fft.rfft(signal, padded_len, axis=0) * jnp.fft.rfft(taps, padded_len)[:, None]
        return jnp.fft.irfft(spectrum, padded_len, axis=0)[:seq_len].astype(jnp.float32)

    grouped = kv_prod.reshape(seq_len, filter_count, group_size).transpose(1, 0, 2)
    conv_out = lax.map(convolve_filter, (grouped, rates, residues))
    conv_out = conv_out.transpose(1, 0, 2).reshape(seq_len, filter_count * group_size)
    hidden = (query * (conv_out + skip_gain[None, :] * kv_prod)).astype(jnp.bfloat16)
    return jnp.dot(hidden, w_out, preferred_element_type=jnp.float32)
```

```python
import functools

import jax
import jax.numpy as jnp
from jax import lax
from jax.experimental import pallas as pl
from jax.experimental.pallas import tpu as pltpu
from jax.sharding import PartitionSpec as P

HIGHEST = lax.Precision.HIGHEST
LANES = 128


def dot_nt(a, b):
    return lax.dot_general(
        a, b, (((1,), (1,)), ((), ())), precision=HIGHEST, preferred_element_type=jnp.float32
    )


def dot_tn(a, b):
    return lax.dot_general(
        a, b, (((0,), (0,)), ((), ())), precision=HIGHEST, preferred_element_type=jnp.float32
    )


def dot_nn(a, b):
    return jnp.dot(a, b, precision=HIGHEST, preferred_element_type=jnp.float32)


def own_filter(modes, rows):
    shape = (LANES // modes, rows, LANES)
    return lax.broadcasted_iota(jnp.int32, shape, 2) // modes == lax.broadcasted_iota(
        jnp.int32, shape, 0
    )


def local_kernel(modes, key_ref, value_ref, rate_ref, res_ref, state_ref, conv_ref):
    tok = key_ref.shape[0]
    filters = LANES // modes
    kv = key_ref[...] * value_ref[...]
    rate = rate_ref[...]
    pos = lax.broadcasted_iota(jnp.int32, (tok, LANES), 0).astype(jnp.float32)
    end = jnp.exp(-rate * (tok - 1.0 - pos))
    full = dot_tn(end, kv).reshape(filters, modes, LANES)
    state_ref[...] = jnp.sum(jnp.where(own_filter(modes, modes), full, 0.0), axis=0)
    centre = pos - tok / 2.0
    rise = res_ref[...] * jnp.exp(rate * centre)
    fall = jnp.exp(-rate * centre)
    mine = own_filter(modes, tok)
    falls = jnp.where(mine, fall[None], 0.0).reshape(filters * tok, LANES)
    taps = dot_nt(falls, rise).reshape(filters, tok, tok)
    shape = (filters, tok, tok)
    causal = lax.broadcasted_iota(jnp.int32, shape, 1) >= lax.broadcasted_iota(jnp.int32, shape, 2)
    taps = jnp.where(causal, taps, 0.0).reshape(filters * tok, tok)
    out = dot_nn(taps, kv).reshape(filters, tok, LANES)
    conv_ref[...] = jnp.sum(jnp.where(mine, out, 0.0), axis=0)


def gate_kernel(
    modes, ctx_count, query_ref, key_ref, value_ref, skip_ref, rate_ref, res_ref, conv_ref,
    rates_nc_ref, states_ref, hidden_ref
):
    tok = key_ref.shape[0]
    filters = LANES // modes
    me = lax.axis_index("ctx")
    carry = jnp.zeros((modes, LANES), jnp.float32)
    decay = jnp.exp(-rates_nc_ref[...] * float(tok))

    def add(j, carry):
        return jnp.where(j < me, carry * decay + states_ref[j], carry)

    carry = lax.fori_loop(0, ctx_count, add, carry)
    spread = jnp.where(
        own_filter(modes, modes), jnp.broadcast_to(carry[None], (filters, modes, LANES)), 0.0
    ).reshape(LANES, LANES)
    pos = lax.broadcasted_iota(jnp.int32, (tok, LANES), 0).astype(jnp.float32)
    out_decay = res_ref[...] * jnp.exp(-rate_ref[...] * (pos + 1.0))
    kv = key_ref[...] * value_ref[...]
    conv = conv_ref[...] + dot_nn(out_decay, spread)
    hidden_ref[...] = (query_ref[...] * (conv + skip_ref[...] * kv)).astype(jnp.bfloat16)


def shards(query, key_proj, value_proj, skip_gain, rates, residues, w_out):
    tok, chan = query.shape
    filters, modes = rates.shape
    width = chan // filters
    ctx_count = lax.axis_size("ctx")
    ch_count = lax.axis_size("ch")
    rate_row = rates.reshape(1, filters * modes)
    res_row = residues.reshape(1, filters * modes)
    rates_nc = jnp.repeat(rates.T, width, axis=1)
    groups = chan // LANES
    wide = pl.BlockSpec((tok, LANES), lambda g: (0, g))
    row = pl.BlockSpec((1, LANES), lambda g: (0, g))
    small = pl.BlockSpec((modes, LANES), lambda g: (0, g))
    state, conv = pl.pallas_call(
        functools.partial(local_kernel, modes),
        grid=(groups,),
        in_specs=[wide, wide, row, row],
        out_specs=[small, wide],
        out_shape=[
            jax.ShapeDtypeStruct((modes, chan), jnp.float32),
            jax.ShapeDtypeStruct((tok, chan), jnp.float32),
        ],
    )(key_proj, value_proj, rate_row, res_row)
    states = lax.all_gather(state, "ctx", axis=0)
    hidden = pl.pallas_call(
        functools.partial(gate_kernel, modes, ctx_count),
        grid=(groups,),
        in_specs=[
            wide, wide, wide, row, row, row, wide, small,
            pl.BlockSpec((ctx_count, modes, LANES), lambda g: (0, 0, g)),
        ],
        out_specs=wide,
        out_shape=jax.ShapeDtypeStruct((tok, chan), jnp.bfloat16),
    )(query, key_proj, value_proj, skip_gain[None], rate_row, res_row, conv, rates_nc, states)
    hidden_all = lax.all_gather(hidden, "ctx", axis=0, tiled=True)
    part = jnp.dot(hidden_all, w_out, preferred_element_type=jnp.float32).astype(jnp.bfloat16)
    part = part.reshape(ctx_count, tok, w_out.shape[1])
    part = lax.all_to_all(part, "ctx", split_axis=0, concat_axis=0)
    part = part.reshape(ch_count, ctx_count // ch_count, tok, w_out.shape[1])
    part = lax.all_to_all(part, "ch", split_axis=0, concat_axis=0)
    total = jnp.sum(part.astype(jnp.float32), axis=0)
    return total.transpose(1, 0, 2).reshape(tok, -1)


def solution(mesh):
    placed = (
        P("ctx", "ch"),
        P("ctx", "ch"),
        P("ctx", "ch"),
        P("ch"),
        P("ch", None),
        P("ch", None),
        P("ch", "ctx"),
    )
    return jax.shard_map(
        shards, mesh=mesh, in_specs=placed, out_specs=P("ctx", "ch"), check_vma=False
    )
```

```python
import functools

import jax
import jax.numpy as jnp
from jax import lax
from jax.experimental import pallas as pl
from jax.experimental.pallas import tpu as pltpu
from jax.sharding import PartitionSpec as P

LANES = 128


MESH = pl.DeviceIdType.MESH


def split3(a, b, dims):
    a_hi, b_hi = a.astype(jnp.bfloat16), b.astype(jnp.bfloat16)
    a_lo = (a - a_hi.astype(jnp.float32)).astype(jnp.bfloat16)
    b_lo = (b - b_hi.astype(jnp.float32)).astype(jnp.bfloat16)

    def one(x, y):
        return lax.dot_general(x, y, (dims, ((), ())), preferred_element_type=jnp.float32)

    return one(a_hi, b_hi) + (one(a_hi, b_lo) + one(a_lo, b_hi))


def dot_nt(a, b):
    return split3(a, b, ((1,), (1,)))


def dot_tn(a, b):
    return split3(a, b, ((0,), (0,)))


def dot_nn(a, b):
    return split3(a, b, ((1,), (0,)))


def own_filter(modes, rows):
    shape = (LANES // modes, rows, LANES)
    return lax.broadcasted_iota(jnp.int32, shape, 2) // modes == lax.broadcasted_iota(
        jnp.int32, shape, 0
    )


def local_kernel(modes, key_ref, value_ref, rate_ref, res_ref, state_ref, conv_ref):
    tok = key_ref.shape[0]
    filters = LANES // modes
    kv = key_ref[...] * value_ref[...]
    rate = rate_ref[...]
    pos = lax.broadcasted_iota(jnp.int32, (tok, LANES), 0).astype(jnp.float32)
    end = jnp.exp(-rate * (tok - 1.0 - pos))
    full = dot_tn(end, kv).reshape(filters, modes, LANES)
    state_ref[...] = jnp.sum(jnp.where(own_filter(modes, modes), full, 0.0), axis=0)
    centre = pos - tok / 2.0
    rise = res_ref[...] * jnp.exp(rate * centre)
    fall = jnp.exp(-rate * centre)
    mine = own_filter(modes, tok)
    falls = jnp.where(mine, fall[None], 0.0).reshape(filters * tok, LANES)
    taps = dot_nt(falls, rise).reshape(filters, tok, tok)
    shape = (filters, tok, tok)
    causal = lax.broadcasted_iota(jnp.int32, shape, 1) >= lax.broadcasted_iota(jnp.int32, shape, 2)
    taps = jnp.where(causal, taps, 0.0).reshape(filters * tok, tok)
    out = dot_nn(taps, kv).reshape(filters, tok, LANES)
    conv_ref[...] = jnp.sum(jnp.where(mine, out, 0.0), axis=0)


def gate_kernel(
    modes, ctx_count, query_ref, key_ref, value_ref, skip_ref, rate_ref, res_ref, conv_ref,
    rates_nc_ref, states_ref, hidden_ref
):
    tok = key_ref.shape[0]
    filters = LANES // modes
    me = lax.axis_index("ctx")
    carry = jnp.zeros((modes, LANES), jnp.float32)
    decay = jnp.exp(-rates_nc_ref[...] * float(tok))

    def add(j, carry):
        return jnp.where(j < me, carry * decay + states_ref[j], carry)

    carry = lax.fori_loop(0, ctx_count, add, carry)
    spread = jnp.where(
        own_filter(modes, modes), jnp.broadcast_to(carry[None], (filters, modes, LANES)), 0.0
    ).reshape(LANES, LANES)
    pos = lax.broadcasted_iota(jnp.int32, (tok, LANES), 0).astype(jnp.float32)
    out_decay = res_ref[...] * jnp.exp(-rate_ref[...] * (pos + 1.0))
    kv = key_ref[...] * value_ref[...]
    conv = conv_ref[...] + dot_nn(out_decay, spread)
    hidden_ref[...] = (query_ref[...] * (conv + skip_ref[...] * kv)).astype(jnp.bfloat16)


def exchange_kernel(
    n, nch, hidden_ref, w_ref, out_ref, held, part, mine, others,
    own_send, pass_send, h_recv, p_send, p_recv, z_send, z_recv
):
    me, my_ch = lax.axis_index("ctx"), lax.axis_index("ch")
    tok = hidden_ref.shape[0]
    cols = w_ref.shape[1]
    per = n // nch
    chips = n // 2
    tile = min(cols, 256)

    def sibling(i):
        return i + 1 - 2 * lax.rem(i, 2)

    sib = sibling(me)

    barrier = pltpu.get_barrier_semaphore()

    def greet_ctx(d, c):
        pl.semaphore_signal(
            barrier, inc=1, device_id={"ctx": lax.rem(me + d, n)}, device_id_type=MESH
        )
        return c

    lax.fori_loop(1, n, greet_ctx, 0)
    for d in range(1, nch):
        pl.semaphore_signal(
            barrier, inc=1, device_id={"ch": lax.rem(my_ch + d, nch)}, device_id_type=MESH
        )
    pl.semaphore_wait(barrier, n + nch - 2)

    def own_copy(d, peer):
        return pltpu.make_async_remote_copy(
            src_ref=hidden_ref, dst_ref=held.at[me], send_sem=own_send.at[d],
            recv_sem=h_recv.at[me], device_id={"ctx": peer}, device_id_type=MESH,
        )

    def pass_copy(d, src):
        return pltpu.make_async_remote_copy(
            src_ref=held.at[src], dst_ref=held.at[src], send_sem=pass_send.at[d],
            recv_sem=h_recv.at[src], device_id={"ctx": sib}, device_id_type=MESH,
        )

    def part_copy(b, t, src):
        return pltpu.make_async_remote_copy(
            src_ref=part.at[t], dst_ref=mine.at[src], send_sem=p_send.at[b],
            recv_sem=p_recv.at[src], device_id={"ctx": t}, device_id_type=MESH,
        )

    def ch_copy(i, to, src_ch):
        slot = lax.rem(i, per)
        return pltpu.make_async_remote_copy(
            src_ref=mine.at[i], dst_ref=others.at[src_ch, slot], send_sem=z_send.at[i],
            recv_sem=z_recv.at[src_ch, slot], device_id={"ch": to}, device_id_type=MESH,
        )

    own_copy(0, sib).start()

    def send_own(d, c):
        own_copy(d, lax.rem(me + 2 * d, n)).start()
        return c

    lax.fori_loop(1, chips, send_own, 0)
    held[me] = hidden_ref[...]

    def block_of(b, sign):
        base = lax.rem(me + sign * 2 * (b // 2) + 2 * n, n)
        odd = lax.rem(b, 2)
        return base + odd * (1 - 2 * lax.rem(base, 2))

    def forward(b):
        i = block_of(b, 1)

        @pl.when(b > 0)
        def _():
            part_copy(b, me, i).wait_recv()

        to = i // per

        @pl.when(to != my_ch)
        def _():
            ch_copy(i, to, my_ch).start()

    def step(b, c):
        t = block_of(b, -1)

        @pl.when(b > 0)
        def _():
            pass_copy(0, t).wait_recv()

        @pl.when(jnp.logical_and(b > 0, lax.rem(b, 2) == 0))
        def _():
            pass_copy(b // 2, t).start()

        for k in range(cols // tile):
            at = pl.ds(k * tile, tile)
            part[t, :, at] = jnp.dot(
                held[t], w_ref[:, at], preferred_element_type=jnp.float32
            ).astype(jnp.bfloat16)

        @pl.when(b > 0)
        def _():
            part_copy(b, t, me).start()

        @pl.when(b == 0)
        def _():
            mine[me] = part[me]

        @pl.when(b > 1)
        def _():
            forward(b - 2)

        return c

    lax.fori_loop(0, n, step, 0)
    forward(n - 2)
    forward(n - 1)

    for slot in range(per):
        i = my_ch * per + slot
        total = mine[i].astype(jnp.float32)
        for d in range(1, nch):
            src_ch = lax.rem(my_ch + d, nch)
            ch_copy(i, src_ch, src_ch).wait_recv()
            total = total + others[src_ch, slot].astype(jnp.float32)
        out_ref[:, slot * cols : (slot + 1) * cols] = total

    own_copy(0, sib).wait_send()

    def drain_own(d, c):
        own_copy(d, sib).wait_send()
        pass_copy(d, me).wait_send()
        return c

    lax.fori_loop(1, chips, drain_own, 0)

    def drain_part(b, c):
        part_copy(b, block_of(b, -1), me).wait_send()
        return c

    lax.fori_loop(1, n, drain_part, 0)

    def drain_ch(i, c):
        @pl.when(i // per != my_ch)
        def _():
            ch_copy(i, i // per, my_ch).wait_send()

        return c

    lax.fori_loop(0, n, drain_ch, 0)


def shards(query, key_proj, value_proj, skip_gain, rates, residues, w_out):
    tok, chan = query.shape
    filters, modes = rates.shape
    width = chan // filters
    ctx_count = lax.axis_size("ctx")
    ch_count = lax.axis_size("ch")
    rate_row = rates.reshape(1, filters * modes)
    res_row = residues.reshape(1, filters * modes)
    rates_nc = jnp.repeat(rates.T, width, axis=1)
    groups = chan // LANES
    wide = pl.BlockSpec((tok, LANES), lambda g: (0, g))
    row = pl.BlockSpec((1, LANES), lambda g: (0, g))
    small = pl.BlockSpec((modes, LANES), lambda g: (0, g))
    state, conv = pl.pallas_call(
        functools.partial(local_kernel, modes),
        grid=(groups,),
        in_specs=[wide, wide, row, row],
        out_specs=[small, wide],
        out_shape=[
            jax.ShapeDtypeStruct((modes, chan), jnp.float32),
            jax.ShapeDtypeStruct((tok, chan), jnp.float32),
        ],
    )(key_proj, value_proj, rate_row, res_row)
    states = lax.all_gather(state, "ctx", axis=0)
    hidden = pl.pallas_call(
        functools.partial(gate_kernel, modes, ctx_count),
        grid=(groups,),
        in_specs=[
            wide, wide, wide, row, row, row, wide, small,
            pl.BlockSpec((ctx_count, modes, LANES), lambda g: (0, 0, g)),
        ],
        out_specs=wide,
        out_shape=jax.ShapeDtypeStruct((tok, chan), jnp.bfloat16),
    )(query, key_proj, value_proj, skip_gain[None], rate_row, res_row, conv, rates_nc, states)
    cols = w_out.shape[1]
    per = ctx_count // ch_count
    block = (tok, cols)
    return pl.pallas_call(
        functools.partial(exchange_kernel, ctx_count, ch_count),
        in_specs=[pl.BlockSpec(memory_space=pltpu.VMEM)] * 2,
        out_specs=pl.BlockSpec(memory_space=pltpu.VMEM),
        out_shape=jax.ShapeDtypeStruct((tok, per * cols), jnp.float32),
        scratch_shapes=[
            pltpu.VMEM((ctx_count, tok, chan), jnp.bfloat16),
            pltpu.VMEM((ctx_count, *block), jnp.bfloat16),
            pltpu.VMEM((ctx_count, *block), jnp.bfloat16),
            pltpu.VMEM((ch_count, per, *block), jnp.bfloat16),
            pltpu.SemaphoreType.DMA((ctx_count // 2,)),
            pltpu.SemaphoreType.DMA((ctx_count // 2,)),
            pltpu.SemaphoreType.DMA((ctx_count,)),
            pltpu.SemaphoreType.DMA((ctx_count,)),
            pltpu.SemaphoreType.DMA((ctx_count,)),
            pltpu.SemaphoreType.DMA((ctx_count,)),
            pltpu.SemaphoreType.DMA((ch_count, per)),
        ],
        compiler_params=pltpu.CompilerParams(
            collective_id=0, has_side_effects=True, vmem_limit_bytes=56 << 20
        ),
    )(hidden, w_out)


def solution(mesh):
    placed = (
        P("ctx", "ch"),
        P("ctx", "ch"),
        P("ctx", "ch"),
        P("ch"),
        P("ch", None),
        P("ch", None),
        P("ch", "ctx"),
    )
    return jax.shard_map(
        shards, mesh=mesh, in_specs=placed, out_specs=P("ctx", "ch"), check_vma=False
    )
```
